512 devices in a mesh: dp: 64 (over y, x, core), fsdp: 8 (over z).
Axes of the slice: x: 4, y: 8, z: 8, core: 2. Of those that a mesh axis runs over, the one named last changes fastest.
Arguments:
- query_emb: bfloat16 [32768, 4096], P('dp', 'fsdp')
- passage_emb: bfloat16 [65536, 4096], P('dp', 'fsdp')
- cand_blocks: int32 [256, 4], P('dp'), may hold values from 0 to 511, as said below
- positive: int32 [32768], P('dp'), may hold values from 0 to 511
Outputs:
- losses: float32 [32768], P(('dp', 'fsdp'))
- query_grad: bfloat16 [32768, 4096], P('dp', 'fsdp')
The draws below stay inside these ranges and needn't reach their ends.
Inputs may be any that keep to these rules, and one draw needn't show every extreme that they name: `cand_blocks`: each query block lists 4 different passage blocks; block b is held by dp index b // 8. The blocks listed by the 4 query blocks of one dp index are all different, at most 1 of them are held by any one dp index, and some dp index holds exactly 1 of them. `positive`: position c names row c % 128 of the block in column c // 128 of the query's list.
All inputs are finite; a program needn't handle non-finite values.
Results may differ from the reference program's by a relative error of at most 0.0038.
Values may be sent and summed in bfloat16 or wider, within the bound.
A program may use at most 64 MiB of HBM per device.

```python
from functools import partial
import jax
import jax.numpy as jnp
from jax import lax

D = 4096
BLK = 128
NLIST = 4
QB_DEV = 4
PB_DEV = 8
QBLOCKS = 256
PBLOCKS = 512
QUERIES = 32768
PASSAGES = 65536
N_DP = 64


def request_ids(key):
    base = jax.random.fold_in(key, 7)
    perm_keys = jax.random.split(jax.random.fold_in(base, 1), N_DP)
    orders = jax.vmap(partial(jax.random.permutation, x=N_DP))(perm_keys)
    request_count = NLIST * QB_DEV
    request_steps = jnp.arange(request_count)
    owners = orders[:, request_steps % N_DP]
    offsets = jax.random.randint(jax.random.fold_in(base, 2), (N_DP, N_DP), 0, PB_DEV)
    local_ids = (jnp.take_along_axis(offsets, owners, axis=1) + request_steps // N_DP) % PB_DEV
    return (owners * PB_DEV + local_ids).reshape(QBLOCKS, NLIST).astype(jnp.int32)


def passage_values(key):
    base = jax.random.fold_in(key, 13)
    values = jax.random.normal(jax.random.fold_in(base, 1), (PASSAGES, D), jnp.float32) * D ** (-0.5)
    return values


def query_values(key):
    base = jax.random.fold_in(key, 29)
    values = jax.random.normal(jax.random.fold_in(base, 1), (QUERIES, D), jnp.float32) * D ** (-0.5)
    return values


def draw_cand_blocks(key, part):
    return request_ids(key)


def draw_passage_emb(key, part):
    return passage_values(key).astype(jnp.bfloat16)


def draw_query_emb(key, part):
    return query_values(key).astype(jnp.bfloat16)


def place_ends(values, key, smallest, high):
    dims = values.shape
    spot = [jax.random.randint(jax.random.fold_in(key, axis), (), 0, dims[axis]) for axis in range(len(dims))]
    values = values.at[tuple(spot)].set(smallest)
    longest = dims.index(max(dims))
    spot[longest] = (spot[longest] + 1) % dims[longest]
    return values.at[tuple(spot)].set(high)


def setup_inputs(seed: int = 0) -> dict:
    streams_of = jax.random.split(jax.random.key(seed), 5)
    return {
        "query_emb": draw_query_emb(jax.random.fold_in(streams_of[4], 71), 0),
        "passage_emb": draw_passage_emb(jax.random.fold_in(streams_of[4], 71), 0),
        "cand_blocks": draw_cand_blocks(jax.random.fold_in(streams_of[4], 71), 0),
        "positive": place_ends(jax.random.randint(streams_of[3], (QUERIES,), 0, NLIST * BLK), jax.random.fold_in(streams_of[3], 1), 0, (NLIST * BLK) - 1).astype(jnp.int32),
    }


def softmax_rows(scores, positive_rows):
    row_max = jnp.max(scores, axis=1, keepdims=True)
    log_total = row_max[:, 0] + jnp.log(jnp.sum(jnp.exp(scores - row_max), axis=1))
    matched = lax.broadcasted_iota(jnp.int32, scores.shape, 1) == positive_rows[:, None]
    losses = log_total - jnp.sum(jnp.where(matched, scores, jnp.float32(0.0)), axis=1)
    weights = (jnp.exp(scores - log_total[:, None]) - matched.astype(jnp.float32)).astype(jnp.bfloat16)
    return losses, weights


def reference(query_emb, passage_emb, cand_blocks, positive):
    passage_blocks = passage_emb.reshape(PBLOCKS, BLK, D)
    query_blocks = query_emb.reshape(QBLOCKS, BLK, D)
    positive_blocks = positive.reshape(QBLOCKS, BLK)

    def one_block(inputs):
        query_rows, listed, positive_rows = inputs
        candidates = passage_blocks[listed].reshape(NLIST * BLK, D)
        scores = jnp.dot(query_rows, candidates.T, preferred_element_type=jnp.float32) * 50.0
        losses, weights = softmax_rows(scores, positive_rows)
        query_grad = (jnp.dot(weights, candidates, preferred_element_type=jnp.float32) * 50.0).astype(jnp.bfloat16)
        return losses, query_grad

    losses, query_grad = lax.map(one_block, (query_blocks, cand_blocks, positive_blocks))
    return losses.reshape(QUERIES), query_grad.reshape(QUERIES, D)
```

```python
import jax
import jax.numpy as jnp
from jax import lax
from jax.experimental import pallas as pl
from jax.experimental.pallas import tpu as pltpu
from jax.sharding import PartitionSpec as P

MESH = pl.DeviceIdType.MESH
RING = 8
ROW = 8


def softmax_rows(scores, positive_rows):
    row_max = jnp.max(scores, axis=1, keepdims=True)
    log_total = row_max[:, 0] + jnp.log(jnp.sum(jnp.exp(scores - row_max), axis=1))
    matched = lax.broadcasted_iota(jnp.int32, scores.shape, 1) == positive_rows[:, None]
    losses = log_total - jnp.sum(jnp.where(matched, scores, jnp.float32(0.0)), axis=1)
    weights = (jnp.exp(scores - log_total[:, None]) - matched.astype(jnp.float32)).astype(
        jnp.bfloat16
    )
    return (losses, weights)


def fetch_kernel(
    slots_ref, table_ref, stored_ref, out_ref,
    r1, r2, r3, l1, l2, l3, far, stage, got, tables, table_smem,
    ring_send, ring_recv, table_send, table_recv, slot_send, slot_recv, local_sem,
):
    me_dp = lax.axis_index("dp")
    y = me_dp // ROW
    member = me_dp % ROW
    up = ((y + 1) % RING) * ROW + member
    down = ((y + RING - 1) % RING) * ROW + member

    def peer_of(k):
        return (member + k) % ROW

    def row_dp(k):
        return y * ROW + peer_of(k)

    barrier = pltpu.get_barrier_semaphore()
    for target in (up, down):
        pl.semaphore_signal(barrier, inc=1, device_id={"dp": target}, device_id_type=MESH)

    def greet(k, carry):
        pl.semaphore_signal(barrier, inc=1, device_id={"dp": row_dp(k)}, device_id_type=MESH)
        return carry

    lax.fori_loop(1, ROW, greet, 0)
    pl.semaphore_wait(barrier, ROW + 1)

    def ring_copy(index, src, dst, target):
        return pltpu.make_async_remote_copy(
            src_ref=src, dst_ref=dst, send_sem=ring_send.at[index], recv_sem=ring_recv.at[index],
            device_id={"dp": target}, device_id_type=MESH,
        )

    half = stored_ref.shape[0] // 2
    rights = [stored_ref, r1, r2, r3]
    lefts = [stored_ref, l1, l2, l3]
    right_copies = [ring_copy(d, rights[d], rights[d + 1], up) for d in range(3)]
    left_copies = [ring_copy(4 + d, lefts[d], lefts[d + 1], down) for d in range(3)]
    first, second = pl.ds(0, half), pl.ds(half, half)
    right_copies.append(ring_copy(3, r3.at[first], far.at[first], up))
    left_copies.append(ring_copy(7, l3.at[second], far.at[second], down))

    right_copies[0].start()
    left_copies[0].start()

    def table_copy(k):
        return pltpu.make_async_remote_copy(
            src_ref=table_ref, dst_ref=tables.at[member],
            send_sem=table_send.at[k], recv_sem=table_recv.at[k],
            device_id={"dp": row_dp(k)}, device_id_type=MESH,
        )

    def start_table(k, carry):
        table_copy(k).start()
        return carry

    def wait_table(k, carry):
        table_copy(k).wait()
        return carry

    lax.fori_loop(1, ROW, start_table, 0)
    own_table = pltpu.make_async_copy(table_ref, tables.at[member], local_sem.at[0])
    own_table.start()
    own_table.wait()
    lax.fori_loop(1, ROW, wait_table, 0)
    to_smem = pltpu.make_async_copy(tables, table_smem, local_sem.at[1])
    to_smem.start()
    to_smem.wait()

    def slot_copy(delta, k):
        return pltpu.make_async_remote_copy(
            src_ref=stage.at[delta, k], dst_ref=got.at[delta * ROW + member],
            send_sem=slot_send.at[delta, k], recv_sem=slot_recv.at[delta, k],
            device_id={"dp": row_dp(k)}, device_id_type=MESH,
        )

    def serve(delta, source):
        owner_y = (y + RING - delta) % RING

        def picked(k):
            chosen = table_smem[peer_of(k), member, owner_y]
            return source[chosen]

        def send_one(k, carry):
            stage[delta, k] = picked(k)
            slot_copy(delta, k).start()
            return carry

        lax.fori_loop(1, ROW, send_one, 0)
        got[delta * ROW + member] = picked(0)

    serve(0, stored_ref)
    for d in range(1, 4):
        right_copies[d - 1].wait_recv()
        right_copies[d].start()
        left_copies[d - 1].wait_recv()
        left_copies[d].start()
        serve(d, rights[d])
        serve(RING - d, lefts[d])
    right_copies[3].wait_recv()
    left_copies[3].wait_recv()
    serve(4, far)

    def wait_slot(index, carry):
        slot_copy(index // (ROW - 1), index % (ROW - 1) + 1).wait()
        return carry

    lax.fori_loop(0, RING * (ROW - 1), wait_slot, 0)
    for copy in right_copies + left_copies:
        copy.wait_send()

    def place(i, carry):
        out_ref[i] = got[slots_ref[i]]
        return carry

    lax.fori_loop(0, out_ref.shape[0], place, 0)


def fetch(slots, table, stored):
    block_rows, features = stored.shape[1:]
    shard = pltpu.VMEM(stored.shape, stored.dtype)
    vmem = pl.BlockSpec(memory_space=pltpu.VMEM)
    return pl.pallas_call(
        fetch_kernel,
        out_shape=jax.ShapeDtypeStruct((slots.shape[0], block_rows, features), stored.dtype),
        in_specs=[pl.BlockSpec(memory_space=pltpu.SMEM), vmem, vmem],
        out_specs=vmem,
        scratch_shapes=[shard] * 7
        + [
            pltpu.VMEM((RING, ROW, block_rows, features), stored.dtype),
            pltpu.VMEM((RING * ROW, block_rows, features), stored.dtype),
            pltpu.VMEM((ROW,) + table.shape, jnp.int32),
            pltpu.SMEM((ROW,) + table.shape, jnp.int32),
            pltpu.SemaphoreType.DMA((8,)),
            pltpu.SemaphoreType.DMA((8,)),
            pltpu.SemaphoreType.DMA((ROW,)),
            pltpu.SemaphoreType.DMA((ROW,)),
            pltpu.SemaphoreType.DMA((RING, ROW)),
            pltpu.SemaphoreType.DMA((RING, ROW)),
            pltpu.SemaphoreType.DMA((2,)),
        ],
        compiler_params=pltpu.CompilerParams(
            collective_id=0, has_side_effects=True, vmem_limit_bytes=48 * 1024 * 1024
        ),
        name="fetch",
    )(slots, table, stored)


def shards(query_emb, passage_emb, cand_blocks, positive):
    fsdp_count = lax.axis_size("fsdp")
    query_blocks, list_len = cand_blocks.shape
    row_count, feature_count = query_emb.shape
    block_rows = row_count // query_blocks
    passage_blocks = passage_emb.shape[0] // block_rows
    wanted = cand_blocks.reshape(-1)
    owners = wanted // passage_blocks
    local_ids = wanted % passage_blocks
    owner_y = owners // ROW
    owner_member = owners % ROW
    at_member = owner_member[:, None, None] == lax.broadcasted_iota(jnp.int32, (1, ROW, 128), 1)
    at_row = owner_y[:, None, None] == lax.broadcasted_iota(jnp.int32, (1, ROW, 128), 2)
    table = jnp.sum(jnp.where(at_member & at_row, local_ids[:, None, None], 0), axis=0)
    my_y = lax.axis_index("dp") // ROW
    slots = ((my_y - owner_y + RING) % RING) * ROW + owner_member
    stored = passage_emb.reshape(passage_blocks, block_rows, feature_count)
    candidates = fetch(slots, table, stored)
    candidates = candidates.reshape(query_blocks, list_len * block_rows, feature_count)
    query_rows = query_emb.reshape(query_blocks, block_rows, feature_count)
    partial_value = jnp.einsum(
        "qnd,qcd->qnc", query_rows, candidates, preferred_element_type=jnp.float32
    )
    partial_value = partial_value.reshape(row_count, list_len * block_rows)
    share_rows = row_count // fsdp_count
    first_row = lax.axis_index("fsdp") * share_rows
    scores = lax.psum(partial_value, "fsdp") * 50.0
    all_losses, weights = softmax_rows(scores, positive)
    losses = lax.dynamic_slice_in_dim(all_losses, first_row, share_rows)
    weights = weights.reshape(query_blocks, block_rows, list_len * block_rows)
    query_grad = (
        jnp.einsum("qnc,qcd->qnd", weights, candidates, preferred_element_type=jnp.float32) * 50.0
    )
    return (losses, query_grad.astype(jnp.bfloat16).reshape(row_count, feature_count))


def solution(mesh):
    return jax.shard_map(
        shards,
        mesh=mesh,
        in_specs=(P("dp", "fsdp"), P("dp", "fsdp"), P("dp", None), P("dp")),
        out_specs=(P(("dp", "fsdp")), P("dp", "fsdp")),
        check_vma=False,
    )
```

```python
import jax
import jax.numpy as jnp
from jax import lax
from jax.experimental import pallas as pl
from jax.experimental.pallas import tpu as pltpu
from jax.sharding import PartitionSpec as P

MESH = pl.DeviceIdType.MESH
RING = 8
ROW = 8
Z = 8


def softmax_rows(scores, positive_rows):
    row_max = jnp.max(scores, axis=1, keepdims=True)
    log_total = row_max + jnp.log(jnp.sum(jnp.exp(scores - row_max), axis=1, keepdims=True))
    matched = lax.broadcasted_iota(jnp.int32, scores.shape, 1) == positive_rows
    losses = log_total - jnp.sum(
        jnp.where(matched, scores, jnp.float32(0.0)), axis=1, keepdims=True
    )
    weights = (jnp.exp(scores - log_total) - matched.astype(jnp.float32)).astype(jnp.bfloat16)
    return (losses, weights)


def loss_kernel(
    slots_ref, table_ref, positive_ref, query_ref, stored_ref, losses_ref, grad_ref,
    r1, r2, r3, l1, l2, l3, far, stage, got, tables, table_smem,
    cands, sums_out, sums_in, weight_own, weight_in, weight_far,
    ring_send, ring_recv, table_send, table_recv, slot_send, slot_recv, local_sem,
    sum_send, sum_recv, weight_send, weight_recv,
):
    me_dp = lax.axis_index("dp")
    y = me_dp // ROW
    member = me_dp % ROW
    up = ((y + 1) % RING) * ROW + member
    down = ((y + RING - 1) % RING) * ROW + member
    z = lax.axis_index("fsdp")
    z_targets = ((z + 1) % Z, (z + Z - 1) % Z)

    def peer_of(k):
        return (member + k) % ROW

    def row_dp(k):
        return y * ROW + peer_of(k)

    barrier = pltpu.get_barrier_semaphore()
    for target in (up, down):
        pl.semaphore_signal(barrier, inc=1, device_id={"dp": target}, device_id_type=MESH)
    for target in z_targets:
        pl.semaphore_signal(barrier, inc=1, device_id={"fsdp": target}, device_id_type=MESH)

    def greet(k, carry):
        pl.semaphore_signal(barrier, inc=1, device_id={"dp": row_dp(k)}, device_id_type=MESH)
        return carry

    lax.fori_loop(1, ROW, greet, 0)
    pl.semaphore_wait(barrier, ROW + 3)

    def ring_copy(index, src, dst, target):
        return pltpu.make_async_remote_copy(
            src_ref=src, dst_ref=dst, send_sem=ring_send.at[index], recv_sem=ring_recv.at[index],
            device_id={"dp": target}, device_id_type=MESH,
        )

    half = stored_ref.shape[0] // 2
    rights = [stored_ref, r1, r2, r3]
    lefts = [stored_ref, l1, l2, l3]
    right_copies = [ring_copy(d, rights[d], rights[d + 1], up) for d in range(3)]
    left_copies = [ring_copy(4 + d, lefts[d], lefts[d + 1], down) for d in range(3)]
    first, second = pl.ds(0, half), pl.ds(half, half)
    right_copies.append(ring_copy(3, r3.at[first], far.at[first], up))
    left_copies.append(ring_copy(7, l3.at[second], far.at[second], down))

    right_copies[0].start()
    left_copies[0].start()

    def table_copy(k):
        return pltpu.make_async_remote_copy(
            src_ref=table_ref, dst_ref=tables.at[member],
            send_sem=table_send.at[k], recv_sem=table_recv.at[k],
            device_id={"dp": row_dp(k)}, device_id_type=MESH,
        )

    def start_table(k, carry):
        table_copy(k).start()
        return carry

    def wait_table(k, carry):
        table_copy(k).wait()
        return carry

    lax.fori_loop(1, ROW, start_table, 0)
    own_table = pltpu.make_async_copy(table_ref, tables.at[member], local_sem.at[0])
    own_table.start()
    own_table.wait()
    lax.fori_loop(1, ROW, wait_table, 0)
    to_smem = pltpu.make_async_copy(tables, table_smem, local_sem.at[1])
    to_smem.start()
    to_smem.wait()

    def slot_copy(delta, k):
        return pltpu.make_async_remote_copy(
            src_ref=stage.at[delta, k], dst_ref=got.at[delta * ROW + member],
            send_sem=slot_send.at[delta, k], recv_sem=slot_recv.at[delta, k],
            device_id={"dp": row_dp(k)}, device_id_type=MESH,
        )

    def serve(delta, source):
        owner_y = (y + RING - delta) % RING

        def picked(k):
            chosen = table_smem[peer_of(k), member, owner_y]
            return source[chosen]

        def send_one(k, carry):
            stage[delta, k] = picked(k)
            slot_copy(delta, k).start()
            return carry

        lax.fori_loop(1, ROW, send_one, 0)
        got[delta * ROW + member] = picked(0)

    serve(0, stored_ref)
    for d in range(1, 4):
        right_copies[d - 1].wait_recv()
        right_copies[d].start()
        left_copies[d - 1].wait_recv()
        left_copies[d].start()
        serve(d, rights[d])
        serve(RING - d, lefts[d])
    right_copies[3].wait_recv()
    left_copies[3].wait_recv()
    serve(4, far)

    def wait_slot(index, carry):
        slot_copy(index // (ROW - 1), index % (ROW - 1) + 1).wait()
        return carry

    lax.fori_loop(0, RING * (ROW - 1), wait_slot, 0)
    for copy in right_copies + left_copies:
        copy.wait_send()

    def place(i, carry):
        cands[i] = got[slots_ref[i]]
        return carry

    lax.fori_loop(0, cands.shape[0], place, 0)

    share, width = weight_own.shape
    features = query_ref.shape[1]
    list_len = width // cands.shape[1]
    half_width, half_share = width // 2, share // 2

    def listed(v):
        return cands[pl.ds((v // 2) * list_len, list_len)].reshape(width, features)

    def rows_of(v):
        return pl.ds(pl.multiple_of(v * share, share), share)

    def partial(offset):
        v = (z + offset) % Z
        value = lax.dot_general(
            query_ref[rows_of(v), :], listed(v), (((1,), (1,)), ((), ())),
            preferred_element_type=jnp.float32,
        )
        return (value[:, :half_width], value[:, half_width:])

    def sum_copy(way, dist, c):
        index = (way, dist - 1, c)
        return pltpu.make_async_remote_copy(
            src_ref=sums_out.at[index], dst_ref=sums_in.at[index],
            send_sem=sum_send.at[index], recv_sem=sum_recv.at[index],
            device_id={"fsdp": z_targets[way]}, device_id_type=MESH,
        )

    copies = []

    def send_sum(way, dist, c, value):
        sums_out[way, dist - 1, c] = value
        copy = sum_copy(way, dist, c)
        copy.start()
        copies.append(copy)

    farthest = partial(4)
    send_sum(0, 4, 0, farthest[0])
    send_sum(1, 4, 1, farthest[1])
    for dist in (3, 2, 1):
        values = (partial(dist), partial(Z - dist))
        order = [(0, 0), (1, 1), (1, 0), (0, 1)]
        if dist == 3:
            order = order[2:] + order[:2]
        for way, c in order:
            value = values[way][c]
            if dist < 3 or way == c:
                sum_copy(way, dist + 1, c).wait_recv()
                value = value + sums_in[way, dist, c]
            send_sum(way, dist, c, value)
    halves = list(partial(0))
    for way, c in ((0, 0), (1, 1), (1, 0), (0, 1)):
        sum_copy(way, 1, c).wait_recv()
        halves[c] = halves[c] + sums_in[way, 0, c]
    scores = jnp.concatenate(halves, axis=1) * 50.0
    losses, weights = softmax_rows(scores, positive_ref[...])
    weight_own[...] = weights
    losses_ref[...] = losses

    def part(ref, c):
        return ref.at[pl.ds(c * half_share, half_share)]

    def weight_copy(way, step, c):
        source = weight_own if step == 0 else weight_in.at[way, step - 1]
        target = weight_far if step == 3 else weight_in.at[way, step]
        return pltpu.make_async_remote_copy(
            src_ref=part(source, c), dst_ref=part(target, c),
            send_sem=weight_send.at[way, step, c], recv_sem=weight_recv.at[way, step, c],
            device_id={"fsdp": z_targets[way]}, device_id_type=MESH,
        )

    def send_weights(way, step, c):
        copy = weight_copy(way, step, c)
        copy.start()
        copies.append(copy)

    def gradient(rows, offset):
        v = (z + offset) % Z
        value = jnp.dot(rows, listed(v), preferred_element_type=jnp.float32) * 50.0
        grad_ref[rows_of(v), :] = value.astype(grad_ref.dtype)

    for c in range(2):
        for way in range(2):
            send_weights(way, 0, c)
    gradient(weights, 0)
    for step in range(1, 4):
        for c in range(2):
            for way in range(2):
                weight_copy(way, step - 1, c).wait_recv()
                if step < 3 or way == c:
                    send_weights(way, step, c)
        gradient(weight_in[0, step - 1], Z - step)
        gradient(weight_in[1, step - 1], step)
    for way in range(2):
        weight_copy(way, 3, way).wait_recv()
    gradient(weight_far[...], 4)
    for copy in copies:
        copy.wait_send()


def loss_and_gradient(slots, table, positive_rows, query, stored):
    block_rows, features = stored.shape[1:]
    share = positive_rows.shape[0]
    width = slots.shape[0] * block_rows * block_rows // query.shape[0]
    vmem = pl.BlockSpec(memory_space=pltpu.VMEM)
    sums = pltpu.VMEM((2, 4, 2, share, width // 2), jnp.float32)
    dma = pltpu.SemaphoreType.DMA
    return pl.pallas_call(
        loss_kernel,
        out_shape=(
            jax.ShapeDtypeStruct((share, 1), jnp.float32),
            jax.ShapeDtypeStruct(query.shape, query.dtype),
        ),
        in_specs=[pl.BlockSpec(memory_space=pltpu.SMEM), vmem, vmem, vmem, vmem],
        out_specs=(vmem, vmem),
        scratch_shapes=[pltpu.VMEM(stored.shape, stored.dtype)] * 7
        + [
            pltpu.VMEM((RING, ROW, block_rows, features), stored.dtype),
            pltpu.VMEM((RING * ROW, block_rows, features), stored.dtype),
            pltpu.VMEM((ROW,) + table.shape, jnp.int32),
            pltpu.SMEM((ROW,) + table.shape, jnp.int32),
            pltpu.VMEM((slots.shape[0], block_rows, features), stored.dtype),
            sums,
            sums,
            pltpu.VMEM((share, width), jnp.bfloat16),
            pltpu.VMEM((2, 3, share, width), jnp.bfloat16),
            pltpu.VMEM((share, width), jnp.bfloat16),
            dma((8,)),
            dma((8,)),
            dma((ROW,)),
            dma((ROW,)),
            dma((RING, ROW)),
            dma((RING, ROW)),
            dma((2,)),
            dma((2, 4, 2)),
            dma((2, 4, 2)),
            dma((2, 4, 2)),
            dma((2, 4, 2)),
        ],
        compiler_params=pltpu.CompilerParams(
            collective_id=0, has_side_effects=True, vmem_limit_bytes=48 * 1024 * 1024
        ),
        name="loss",
    )(slots, table, positive_rows, query, stored)


def shards(query_emb, passage_emb, cand_blocks, positive):
    row_count, feature_count = query_emb.shape
    block_rows = row_count // cand_blocks.shape[0]
    passage_blocks = passage_emb.shape[0] // block_rows
    wanted = cand_blocks.reshape(-1)
    owners = wanted // passage_blocks
    local_ids = wanted % passage_blocks
    owner_y = owners // ROW
    owner_member = owners % ROW
    at_member = owner_member[:, None, None] == lax.broadcasted_iota(jnp.int32, (1, ROW, 128), 1)
    at_row = owner_y[:, None, None] == lax.broadcasted_iota(jnp.int32, (1, ROW, 128), 2)
    table = jnp.sum(jnp.where(at_member & at_row, local_ids[:, None, None], 0), axis=0)
    my_y = lax.axis_index("dp") // ROW
    slots = ((my_y - owner_y + RING) % RING) * ROW + owner_member
    share = row_count // Z
    first_row = lax.axis_index("fsdp") * share
    positive_rows = lax.dynamic_slice_in_dim(positive, first_row, share)[:, None]
    stored = passage_emb.reshape(passage_blocks, block_rows, feature_count)
    losses, query_grad = loss_and_gradient(slots, table, positive_rows, query_emb, stored)
    return (losses[:, 0], query_grad)


def solution(mesh):
    return jax.shard_map(
        shards,
        mesh=mesh,
        in_specs=(P("dp", "fsdp"), P("dp", "fsdp"), P("dp", None), P("dp")),
        out_specs=(P(("dp", "fsdp")), P("dp", "fsdp")),
        check_vma=False,
    )
```

```python
import jax
import jax.numpy as jnp
from jax import lax
from jax.experimental import pallas as pl
from jax.experimental.pallas import tpu as pltpu
from jax.sharding import PartitionSpec as P

MESH = pl.DeviceIdType.MESH
RING = 8
ROW = 8
Z = 8
CHUNKS = 2


def softmax_rows(scores, positive_rows):
    row_max = jnp.max(scores, axis=1, keepdims=True)
    log_total = row_max + jnp.log(jnp.sum(jnp.exp(scores - row_max), axis=1, keepdims=True))
    matched = lax.broadcasted_iota(jnp.int32, scores.shape, 1) == positive_rows
    losses = log_total - jnp.sum(
        jnp.where(matched, scores, jnp.float32(0.0)), axis=1, keepdims=True
    )
    weights = (jnp.exp(scores - log_total) - matched.astype(jnp.float32)).astype(jnp.bfloat16)
    return (losses, weights)


def loss_kernel(
    slots_ref, table_ref, positive_ref, query_hbm, stored_hbm, losses_ref, grad_ref,
    *scratch,
):
    travelling = scratch[: 7 * CHUNKS]
    (
        query_ref, stored_ref, stage, got, tables, table_smem,
        cands, sums_out, sums_in, weight_own, weight_in, weight_far,
        ring_send, ring_recv, table_send, table_recv, slot_send, slot_recv, local_sem,
        sum_send, sum_recv, weight_send, weight_recv,
    ) = scratch[7 * CHUNKS :]
    load_query = pltpu.make_async_copy(query_hbm, query_ref, local_sem.at[2])
    load_stored = pltpu.make_async_copy(stored_hbm, stored_ref, local_sem.at[3])
    load_stored.start()
    me_dp = lax.axis_index("dp")
    y = me_dp // ROW
    member = me_dp % ROW
    up = ((y + 1) % RING) * ROW + member
    down = ((y + RING - 1) % RING) * ROW + member
    z = lax.axis_index("fsdp")
    z_targets = ((z + 1) % Z, (z + Z - 1) % Z)

    def peer_of(k):
        return (member + k) % ROW

    def row_dp(k):
        return y * ROW + peer_of(k)

    barrier = pltpu.get_barrier_semaphore()
    for target in (up, down):
        pl.semaphore_signal(barrier, inc=1, device_id={"dp": target}, device_id_type=MESH)
    for target in z_targets:
        pl.semaphore_signal(barrier, inc=1, device_id={"fsdp": target}, device_id_type=MESH)

    def greet(k, carry):
        pl.semaphore_signal(barrier, inc=1, device_id={"dp": row_dp(k)}, device_id_type=MESH)
        return carry

    lax.fori_loop(1, ROW, greet, 0)
    pl.semaphore_wait(barrier, ROW + 3)

    chunk = stored_ref.shape[1] // CHUNKS

    def arrived(way, c, d):
        if d == 0:
            return stored_hbm.at[:, pl.ds(c * chunk, chunk)]
        return travelling[6 * CHUNKS + c if d == 4 else (3 * way + d - 1) * CHUNKS + c]

    def ring_copy(way, c, d):
        return pltpu.make_async_remote_copy(
            src_ref=arrived(way, c, d), dst_ref=arrived(way, c, d + 1),
            send_sem=ring_send.at[way, c, d], recv_sem=ring_recv.at[way, c, d],
            device_id={"dp": (up, down)[way]}, device_id_type=MESH,
        )

    def passes(way, c, d):
        return d < 3 or (d == 3 and c % 2 == way)

    ring_copies = []

    def pass_on(way, c, d):
        if passes(way, c, d):
            ring_copies.append(ring_copy(way, c, d))
            ring_copies[-1].start()

    for c in range(CHUNKS):
        for way in range(2):
            pass_on(way, c, 0)
    load_query.start()

    def table_copy(k):
        return pltpu.make_async_remote_copy(
            src_ref=table_ref, dst_ref=tables.at[member],
            send_sem=table_send.at[k], recv_sem=table_recv.at[k],
            device_id={"dp": row_dp(k)}, device_id_type=MESH,
        )

    def start_table(k, carry):
        table_copy(k).start()
        return carry

    def wait_table(k, carry):
        table_copy(k).wait()
        return carry

    lax.fori_loop(1, ROW, start_table, 0)
    own_table = pltpu.make_async_copy(table_ref, tables.at[member], local_sem.at[0])
    own_table.start()
    lax.fori_loop(1, ROW, wait_table, 0)
    own_table.wait()
    to_smem = pltpu.make_async_copy(tables, table_smem, local_sem.at[1])
    to_smem.start()
    to_smem.wait()

    def slot_copy(delta, c, k):
        rows = pl.ds(c * chunk, chunk)
        return pltpu.make_async_remote_copy(
            src_ref=stage.at[delta, k, rows], dst_ref=got.at[delta * ROW + member, rows],
            send_sem=slot_send.at[delta, c, k], recv_sem=slot_recv.at[delta, c, k],
            device_id={"dp": row_dp(k)}, device_id_type=MESH,
        )

    def serve(delta, c, picked_from):
        owner_y = (y + RING - delta) % RING
        rows = pl.ds(c * chunk, chunk)

        def picked(k):
            return picked_from(table_smem[peer_of(k), member, owner_y])

        def send_one(k, carry):
            stage[delta, k, rows] = picked(k)
            slot_copy(delta, c, k).start()
            return carry

        lax.fori_loop(1, ROW, send_one, 0)
        got[delta * ROW + member, rows] = picked(0)

    load_stored.wait()
    for c in range(CHUNKS):
        serve(0, c, lambda chosen: stored_ref[chosen, pl.ds(c * chunk, chunk)])
    for d in range(1, 5):
        for c in range(CHUNKS):
            ways = [way for way in range(2) if passes(way, c, d - 1)]
            for way in ways:
                ring_copy(way, c, d - 1).wait_recv()
                pass_on(way, c, d)
            for way in ways:
                source = arrived(way, c, d)
                serve(RING - d if way else d, c, lambda chosen: source[chosen])

    for c in range(CHUNKS):

        def wait_slot(index, carry):
            slot_copy(index // (ROW - 1), c, index % (ROW - 1) + 1).wait()
            return carry

        lax.fori_loop(0, RING * (ROW - 1), wait_slot, 0)
    for copy in ring_copies:
        copy.wait_send()
    load_query.wait()

    def place(i, carry):
        cands[i] = got[slots_ref[i]]
        return carry

    lax.fori_loop(0, cands.shape[0], place, 0)

    share, width = weight_own.shape
    features = query_ref.shape[1]
    list_len = width // cands.shape[1]
    half_width, half_share = width // 2, share // 2

    def listed(v):
        return cands[pl.ds((v // 2) * list_len, list_len)].reshape(width, features)

    def rows_of(v):
        return pl.ds(pl.multiple_of(v * share, share), share)

    def partial(offset):
        v = (z + offset) % Z
        value = lax.dot_general(
            query_ref[rows_of(v), :], listed(v), (((1,), (1,)), ((), ())),
            preferred_element_type=jnp.float32,
        )
        return (value[:, :half_width], value[:, half_width:])

    def sum_copy(way, dist, c):
        index = (way, dist - 1, c)
        return pltpu.make_async_remote_copy(
            src_ref=sums_out.at[index], dst_ref=sums_in.at[index],
            send_sem=sum_send.at[index], recv_sem=sum_recv.at[index],
            device_id={"fsdp": z_targets[way]}, device_id_type=MESH,
        )

    copies = []

    def send_sum(way, dist, c, value):
        sums_out[way, dist - 1, c] = value
        copy = sum_copy(way, dist, c)
        copy.start()
        copies.append(copy)

    farthest = partial(4)
    send_sum(0, 4, 0, farthest[0])
    send_sum(1, 4, 1, farthest[1])
    for dist in (3, 2, 1):
        values = (partial(dist), partial(Z - dist))
        order = [(0, 0), (1, 1), (1, 0), (0, 1)]
        if dist == 3:
            order = order[2:] + order[:2]
        for way, c in order:
            value = values[way][c]
            if dist < 3 or way == c:
                sum_copy(way, dist + 1, c).wait_recv()
                value = value + sums_in[way, dist, c]
            send_sum(way, dist, c, value)
    halves = list(partial(0))
    for way, c in ((0, 0), (1, 1), (1, 0), (0, 1)):
        sum_copy(way, 1, c).wait_recv()
        halves[c] = halves[c] + sums_in[way, 0, c]
    scores = jnp.concatenate(halves, axis=1) * 50.0
    losses, weights = softmax_rows(scores, positive_ref[...])
    weight_own[...] = weights
    losses_ref[...] = losses

    def part(ref, c):
        return ref.at[pl.ds(c * half_share, half_share)]

    def weight_copy(way, step, c):
        source = weight_own if step == 0 else weight_in.at[way, step - 1]
        target = weight_far if step == 3 else weight_in.at[way, step]
        return pltpu.make_async_remote_copy(
            src_ref=part(source, c), dst_ref=part(target, c),
            send_sem=weight_send.at[way, step, c], recv_sem=weight_recv.at[way, step, c],
            device_id={"fsdp": z_targets[way]}, device_id_type=MESH,
        )

    def send_weights(way, step, c):
        copy = weight_copy(way, step, c)
        copy.start()
        copies.append(copy)

    def gradient(rows, offset):
        v = (z + offset) % Z
        value = jnp.dot(rows, listed(v), preferred_element_type=jnp.float32) * 50.0
        grad_ref[rows_of(v), :] = value.astype(grad_ref.dtype)

    for c in range(2):
        for way in range(2):
            send_weights(way, 0, c)
    gradient(weights, 0)
    for step in range(1, 4):
        for c in range(2):
            for way in range(2):
                weight_copy(way, step - 1, c).wait_recv()
                if step < 3 or way == c:
                    send_weights(way, step, c)
        gradient(weight_in[0, step - 1], Z - step)
        gradient(weight_in[1, step - 1], step)
    for way in range(2):
        weight_copy(way, 3, way).wait_recv()
    gradient(weight_far[...], 4)
    for copy in copies:
        copy.wait_send()


def loss_and_gradient(slots, table, positive_rows, query, stored):
    block_rows, features = stored.shape[1:]
    share = positive_rows.shape[0]
    width = slots.shape[0] * block_rows * block_rows // query.shape[0]
    vmem = pl.BlockSpec(memory_space=pltpu.VMEM)
    hbm = pl.BlockSpec(memory_space=pltpu.HBM)
    travelling = pltpu.VMEM(
        (stored.shape[0], block_rows // CHUNKS, features), stored.dtype
    )
    sums = pltpu.VMEM((2, 4, 2, share, width // 2), jnp.float32)
    dma = pltpu.SemaphoreType.DMA
    return pl.pallas_call(
        loss_kernel,
        out_shape=(
            jax.ShapeDtypeStruct((share, 1), jnp.float32),
            jax.ShapeDtypeStruct(query.shape, query.dtype),
        ),
        in_specs=[pl.BlockSpec(memory_space=pltpu.SMEM), vmem, vmem, hbm, hbm],
        out_specs=(vmem, vmem),
        scratch_shapes=[travelling] * (7 * CHUNKS)
        + [
            pltpu.VMEM(query.shape, query.dtype),
            pltpu.VMEM(stored.shape, stored.dtype),
            pltpu.VMEM((RING, ROW, block_rows, features), stored.dtype),
            pltpu.VMEM((RING * ROW, block_rows, features), stored.dtype),
            pltpu.VMEM((ROW,) + table.shape, jnp.int32),
            pltpu.SMEM((ROW,) + table.shape, jnp.int32),
            pltpu.VMEM((slots.shape[0], block_rows, features), stored.dtype),
            sums,
            sums,
            pltpu.VMEM((share, width), jnp.bfloat16),
            pltpu.VMEM((2, 3, share, width), jnp.bfloat16),
            pltpu.VMEM((share, width), jnp.bfloat16),
            dma((2, CHUNKS, 4)),
            dma((2, CHUNKS, 4)),
            dma((ROW,)),
            dma((ROW,)),
            dma((RING, CHUNKS, ROW)),
            dma((RING, CHUNKS, ROW)),
            dma((4,)),
            dma((2, 4, 2)),
            dma((2, 4, 2)),
            dma((2, 4, 2)),
            dma((2, 4, 2)),
        ],
        compiler_params=pltpu.CompilerParams(
            collective_id=0, has_side_effects=True, vmem_limit_bytes=48 * 1024 * 1024
        ),
        name="loss",
    )(slots, table, positive_rows, query, stored)


def shards(query_emb, passage_emb, cand_blocks, positive):
    row_count, feature_count = query_emb.shape
    block_rows = row_count // cand_blocks.shape[0]
    passage_blocks = passage_emb.shape[0] // block_rows
    wanted = cand_blocks.reshape(-1)
    owners = wanted // passage_blocks
    local_ids = wanted % passage_blocks
    owner_y = owners // ROW
    owner_member = owners % ROW
    at_member = owner_member[:, None, None] == lax.broadcasted_iota(jnp.int32, (1, ROW, 128), 1)
    at_row = owner_y[:, None, None] == lax.broadcasted_iota(jnp.int32, (1, ROW, 128), 2)
    table = jnp.sum(jnp.where(at_member & at_row, local_ids[:, None, None], 0), axis=0)
    my_y = lax.axis_index("dp") // ROW
    slots = ((my_y - owner_y + RING) % RING) * ROW + owner_member
    share = row_count // Z
    first_row = lax.axis_index("fsdp") * share
    positive_rows = lax.dynamic_slice_in_dim(positive, first_row, share)[:, None]
    stored = passage_emb.reshape(passage_blocks, block_rows, feature_count)
    losses, query_grad = loss_and_gradient(slots, table, positive_rows, query_emb, stored)
    return (losses[:, 0], query_grad)


def solution(mesh):
    return jax.shard_map(
        shards,
        mesh=mesh,
        in_specs=(P("dp", "fsdp"), P("dp", "fsdp"), P("dp", None), P("dp")),
        out_specs=(P(("dp", "fsdp")), P("dp", "fsdp")),
        check_vma=False,
    )
```

```python
import jax
import jax.numpy as jnp
from jax import lax
from jax.experimental import pallas as pl
from jax.experimental.pallas import tpu as pltpu
from jax.sharding import PartitionSpec as P

MESH = pl.DeviceIdType.MESH
RING = 8
ROW = 8
Z = 8
CHUNKS = 2
PIECES = 2


def softmax_rows(scores, matched):
    row_max = jnp.max(scores, axis=1, keepdims=True)
    log_total = row_max + jnp.log(jnp.sum(jnp.exp(scores - row_max), axis=1, keepdims=True))
    losses = log_total - jnp.sum(
        jnp.where(matched, scores, jnp.float32(0.0)), axis=1, keepdims=True
    )
    weights = (jnp.exp(scores - log_total) - matched.astype(jnp.float32)).astype(jnp.bfloat16)
    return (losses, weights)


def loss_kernel(
    slots_ref, table_ref, positive_ref, query_hbm, stored_hbm, losses_ref, grad_ref,
    *scratch,
):
    travelling = scratch[: 7 * CHUNKS]
    (
        query_ref, stored_ref, stage, got0, got1, tables, table_smem,
        cands0, cands1, sums_out, sums_in, weight_own, weight_in, weight_far,
        ring_send, ring_recv, table_send, table_recv, slot_send, slot_recv, local_sem,
        sum_send, sum_recv, weight_send, weight_recv,
    ) = scratch[7 * CHUNKS :]
    got, cands = (got0, got1), (cands0, cands1)
    load_query = pltpu.make_async_copy(query_hbm, query_ref, local_sem.at[2])
    load_stored = pltpu.make_async_copy(stored_hbm, stored_ref, local_sem.at[3])
    load_stored.start()
    me_dp = lax.axis_index("dp")
    y = me_dp // ROW
    member = me_dp % ROW
    up = ((y + 1) % RING) * ROW + member
    down = ((y + RING - 1) % RING) * ROW + member
    z = lax.axis_index("fsdp")
    z_targets = ((z + 1) % Z, (z + Z - 1) % Z)

    def peer_of(k):
        return (member + k) % ROW

    def row_dp(k):
        return y * ROW + peer_of(k)

    barrier = pltpu.get_barrier_semaphore()
    for target in (up, down):
        pl.semaphore_signal(barrier, inc=1, device_id={"dp": target}, device_id_type=MESH)
    for target in z_targets:
        pl.semaphore_signal(barrier, inc=1, device_id={"fsdp": target}, device_id_type=MESH)

    def greet(k, carry):
        pl.semaphore_signal(barrier, inc=1, device_id={"dp": row_dp(k)}, device_id_type=MESH)
        return carry

    lax.fori_loop(1, ROW, greet, 0)
    pl.semaphore_wait(barrier, ROW + 3)

    chunk = stored_ref.shape[1] // CHUNKS
    piece = chunk // PIECES

    def arrived(way, c, d):
        return travelling[6 * CHUNKS + c if d == 4 else (3 * way + d - 1) * CHUNKS + c]

    def piece_of(way, c, p, d):
        if d == 0:
            return stored_hbm.at[:, pl.ds(c * chunk + p * piece, piece)]
        return arrived(way, c, d).at[:, pl.ds(p * piece, piece)]

    def ring_copy(way, c, p, d):
        return pltpu.make_async_remote_copy(
            src_ref=piece_of(way, c, p, d), dst_ref=piece_of(way, c, p, d + 1),
            send_sem=ring_send.at[way, c, p, d], recv_sem=ring_recv.at[way, c, p, d],
            device_id={"dp": (up, down)[way]}, device_id_type=MESH,
        )

    def passes(way, p, d):
        return d < 3 or (d == 3 and p == way)

    ring_copies = []

    def pass_on(way, c, p, d):
        if passes(way, p, d):
            ring_copies.append(ring_copy(way, c, p, d))
            ring_copies[-1].start()

    def set_out(c):
        for p in range(PIECES):
            for way in range(2):
                pass_on(way, c, p, 0)

    def table_copy(k):
        return pltpu.make_async_remote_copy(
            src_ref=table_ref, dst_ref=tables.at[member],
            send_sem=table_send.at[k], recv_sem=table_recv.at[k],
            device_id={"dp": row_dp(k)}, device_id_type=MESH,
        )

    def start_table(k, carry):
        table_copy(k).start()
        return carry

    lax.fori_loop(1, ROW, start_table, 0)
    own_table = pltpu.make_async_copy(table_ref, tables.at[member], local_sem.at[0])
    own_table.start()
    set_out(0)
    load_query.start()

    def wait_table(k, carry):
        table_copy(k).wait()
        return carry

    lax.fori_loop(1, ROW, wait_table, 0)
    own_table.wait()
    to_smem = pltpu.make_async_copy(tables, table_smem, local_sem.at[1])
    to_smem.start()
    to_smem.wait()

    def slot_copy(delta, c, k):
        return pltpu.make_async_remote_copy(
            src_ref=stage.at[delta, k, pl.ds(c * chunk, chunk)],
            dst_ref=got[c].at[delta * ROW + member],
            send_sem=slot_send.at[delta, c, k], recv_sem=slot_recv.at[delta, c, k],
            device_id={"dp": row_dp(k)}, device_id_type=MESH,
        )

    def serve(delta, c, picked_from):
        owner_y = (y + RING - delta) % RING

        def picked(k):
            return picked_from(table_smem[peer_of(k), member, owner_y])

        def send_one(k, carry):
            stage[delta, k, pl.ds(c * chunk, chunk)] = picked(k)
            slot_copy(delta, c, k).start()
            return carry

        lax.fori_loop(1, ROW, send_one, 0)
        got[c][delta * ROW + member] = picked(0)

    share, width = weight_own.shape
    features = query_ref.shape[1]
    list_len = width // (CHUNKS * chunk)
    part_width = width // CHUNKS
    half_width, half_share = part_width // 2, share // 2
    copies = []

    def collect(c):
        def wait_slot(index, carry):
            slot_copy(index // (ROW - 1), c, index % (ROW - 1) + 1).wait()
            return carry

        def place(i, carry):
            cands[c][i] = got[c][slots_ref[i]]
            return carry

        lax.fori_loop(0, RING * (ROW - 1), wait_slot, 0)
        lax.fori_loop(0, cands[c].shape[0], place, 0)

    def listed(v, c):
        return cands[c][pl.ds((v // 2) * list_len, list_len)].reshape(part_width, features)

    def rows_of(v):
        return pl.ds(pl.multiple_of(v * share, share), share)

    def partial(c, offset):
        v = (z + offset) % Z
        value = lax.dot_general(
            query_ref[rows_of(v), :], listed(v, c), (((1,), (1,)), ((), ())),
            preferred_element_type=jnp.float32,
        )
        return (value[:, :half_width], value[:, half_width:])

    def sum_copy(c, way, dist, half):
        index = (c, way, dist - 1, half)
        return pltpu.make_async_remote_copy(
            src_ref=sums_out.at[index], dst_ref=sums_in.at[index],
            send_sem=sum_send.at[index], recv_sem=sum_recv.at[index],
            device_id={"fsdp": z_targets[way]}, device_id_type=MESH,
        )

    def send_sum(c, way, dist, half, value):
        sums_out[c, way, dist - 1, half] = value
        copies.append(sum_copy(c, way, dist, half))
        copies[-1].start()

    order = [(0, 0), (1, 1), (1, 0), (0, 1)]

    def sum_step(c, dist):
        values = (partial(c, dist), partial(c, Z - dist) if dist < 4 else None)
        if dist == 4:
            send_sum(c, 0, 4, 0, values[0][0])
            send_sum(c, 1, 4, 1, values[0][1])
            return
        for way, half in order[2:] + order[:2] if dist == 3 else order:
            value = values[way][half]
            if dist < 3 or way == half:
                sum_copy(c, way, dist + 1, half).wait_recv()
                value = value + sums_in[c, way, dist, half]
            send_sum(c, way, dist, half, value)

    def sum_end(c):
        halves = list(partial(c, 0))
        for way, half in order:
            sum_copy(c, way, 1, half).wait_recv()
            halves[half] = halves[half] + sums_in[c, way, 0, half]
        return halves

    load_stored.wait()
    for c in range(CHUNKS):
        serve(0, c, lambda chosen: stored_ref[chosen, pl.ds(c * chunk, chunk)])
    for c in range(CHUNKS):
        for d in range(1, 5):
            for p in range(PIECES):
                for way in range(2):
                    if passes(way, p, d - 1):
                        ring_copy(way, c, p, d - 1).wait_recv()
                        pass_on(way, c, p, d)
            if c == 0 and d == 3:
                set_out(1)
            for way in range(2 if d < 4 else 1):
                source = arrived(way, c, d)
                serve(RING - d if way else d, c, lambda chosen: source[chosen])
            if c == 1 and d == 2:
                load_query.wait()
                collect(0)
                sum_step(0, 4)
            if c == 1 and d == 3:
                sum_step(0, 3)
    sum_step(0, 2)
    sum_step(0, 1)
    halves = sum_end(0)
    collect(1)
    for dist in (4, 3, 2, 1):
        sum_step(1, dist)
    scores = jnp.concatenate(halves + sum_end(1), axis=1) * 50.0
    column = lax.broadcasted_iota(jnp.int32, scores.shape, 1)
    position = (
        (column % part_width // chunk) * (CHUNKS * chunk)
        + (column // part_width) * chunk
        + column % chunk
    )
    losses, weights = softmax_rows(scores, position == positive_ref[...])
    weight_own[...] = weights
    losses_ref[...] = losses

    def part(ref, c):
        return ref.at[pl.ds(c * half_share, half_share)]

    def weight_copy(way, step, c):
        source = weight_own if step == 0 else weight_in.at[way, step - 1]
        target = weight_far if step == 3 else weight_in.at[way, step]
        return pltpu.make_async_remote_copy(
            src_ref=part(source, c), dst_ref=part(target, c),
            send_sem=weight_send.at[way, step, c], recv_sem=weight_recv.at[way, step, c],
            device_id={"fsdp": z_targets[way]}, device_id_type=MESH,
        )

    def send_weights(way, step, c):
        copy = weight_copy(way, step, c)
        copy.start()
        copies.append(copy)

    def gradient(rows, offset):
        v = (z + offset) % Z
        value = sum(
            jnp.dot(
                rows[:, c * part_width : (c + 1) * part_width], listed(v, c),
                preferred_element_type=jnp.float32,
            )
            for c in range(CHUNKS)
        )
        grad_ref[rows_of(v), :] = (value * 50.0).astype(grad_ref.dtype)

    for c in range(2):
        for way in range(2):
            send_weights(way, 0, c)
    gradient(weights, 0)
    for step in range(1, 4):
        for c in range(2):
            for way in range(2):
                weight_copy(way, step - 1, c).wait_recv()
                if step < 3 or way == c:
                    send_weights(way, step, c)
        gradient(weight_in[0, step - 1], Z - step)
        gradient(weight_in[1, step - 1], step)
    for way in range(2):
        weight_copy(way, 3, way).wait_recv()
    gradient(weight_far[...], 4)
    for copy in copies + ring_copies:
        copy.wait_send()


def loss_and_gradient(slots, table, positive_rows, query, stored):
    block_rows, features = stored.shape[1:]
    share = positive_rows.shape[0]
    width = slots.shape[0] * block_rows * block_rows // query.shape[0]
    vmem = pl.BlockSpec(memory_space=pltpu.VMEM)
    hbm = pl.BlockSpec(memory_space=pltpu.HBM)
    travelling = pltpu.VMEM(
        (stored.shape[0], block_rows // CHUNKS, features), stored.dtype
    )
    chunk = block_rows // CHUNKS
    sums = pltpu.VMEM((CHUNKS, 2, 4, 2, share, width // CHUNKS // 2), jnp.float32)
    dma = pltpu.SemaphoreType.DMA
    return pl.pallas_call(
        loss_kernel,
        out_shape=(
            jax.ShapeDtypeStruct((share, 1), jnp.float32),
            jax.ShapeDtypeStruct(query.shape, query.dtype),
        ),
        in_specs=[pl.BlockSpec(memory_space=pltpu.SMEM), vmem, vmem, hbm, hbm],
        out_specs=(vmem, vmem),
        scratch_shapes=[travelling] * (7 * CHUNKS)
        + [
            pltpu.VMEM(query.shape, query.dtype),
            pltpu.VMEM(stored.shape, stored.dtype),
            pltpu.VMEM((RING, ROW, block_rows, features), stored.dtype),
            pltpu.VMEM((RING * ROW, chunk, features), stored.dtype),
            pltpu.VMEM((RING * ROW, chunk, features), stored.dtype),
            pltpu.VMEM((ROW,) + table.shape, jnp.int32),
            pltpu.SMEM((ROW,) + table.shape, jnp.int32),
            pltpu.VMEM((slots.shape[0], chunk, features), stored.dtype),
            pltpu.VMEM((slots.shape[0], chunk, features), stored.dtype),
            sums,
            sums,
            pltpu.VMEM((share, width), jnp.bfloat16),
            pltpu.VMEM((2, 3, share, width), jnp.bfloat16),
            pltpu.VMEM((share, width), jnp.bfloat16),
            dma((2, CHUNKS, PIECES, 4)),
            dma((2, CHUNKS, PIECES, 4)),
            dma((ROW,)),
            dma((ROW,)),
            dma((RING, CHUNKS, ROW)),
            dma((RING, CHUNKS, ROW)),
            dma((4,)),
            dma((CHUNKS, 2, 4, 2)),
            dma((CHUNKS, 2, 4, 2)),
            dma((2, 4, 2)),
            dma((2, 4, 2)),
        ],
        compiler_params=pltpu.CompilerParams(
            collective_id=0, has_side_effects=True, vmem_limit_bytes=48 * 1024 * 1024
        ),
        name="loss",
    )(slots, table, positive_rows, query, stored)


def shards(query_emb, passage_emb, cand_blocks, positive):
    row_count, feature_count = query_emb.shape
    block_rows = row_count // cand_blocks.shape[0]
    passage_blocks = passage_emb.shape[0] // block_rows
    wanted = cand_blocks.reshape(-1)
    owners = wanted // passage_blocks
    local_ids = wanted % passage_blocks
    owner_y = owners // ROW
    owner_member = owners % ROW
    at_member = owner_member[:, None, None] == lax.broadcasted_iota(jnp.int32, (1, ROW, 128), 1)
    at_row = owner_y[:, None, None] == lax.broadcasted_iota(jnp.int32, (1, ROW, 128), 2)
    table = jnp.sum(jnp.where(at_member & at_row, local_ids[:, None, None], 0), axis=0)
    my_y = lax.axis_index("dp") // ROW
    slots = ((my_y - owner_y + RING) % RING) * ROW + owner_member
    share = row_count // Z
    first_row = lax.axis_index("fsdp") * share
    positive_rows = lax.dynamic_slice_in_dim(positive, first_row, share)[:, None]
    stored = passage_emb.reshape(passage_blocks, block_rows, feature_count)
    losses, query_grad = loss_and_gradient(slots, table, positive_rows, query_emb, stored)
    return (losses[:, 0], query_grad)


def solution(mesh):
    return jax.shard_map(
        shards,
        mesh=mesh,
        in_specs=(P("dp", "fsdp"), P("dp", "fsdp"), P("dp", None), P("dp")),
        out_specs=(P(("dp", "fsdp")), P("dp", "fsdp")),
        check_vma=False,
    )
```

```python
import jax
import jax.numpy as jnp
from jax import lax
from jax.experimental import pallas as pl
from jax.experimental.pallas import tpu as pltpu
from jax.sharding import PartitionSpec as P

MESH = pl.DeviceIdType.MESH
RING = 8
ROW = 8
Z = 8
CHUNKS = 2
PIECES = 2


def softmax_rows(scores, matched):
    row_max = jnp.max(scores, axis=1, keepdims=True)
    log_total = row_max + jnp.log(jnp.sum(jnp.exp(scores - row_max), axis=1, keepdims=True))
    losses = log_total - jnp.sum(
        jnp.where(matched, scores, jnp.float32(0.0)), axis=1, keepdims=True
    )
    weights = (jnp.exp(scores - log_total) - matched.astype(jnp.float32)).astype(jnp.bfloat16)
    return (losses, weights)


def loss_kernel(
    slots_ref, table_ref, positive_ref, query_hbm, stored_hbm, losses_ref, grad_ref,
    *scratch,
):
    travelling = scratch[: 7 * CHUNKS]
    (
        query_ref, stored_ref, stage, got0, got1, tables, table_smem,
        cands0, cands1, sums_out, sums_in, weight_own, weight_in, weight_far,
        ring_send, ring_recv, table_send, table_recv, slot_send, slot_recv, local_sem,
        sum_send, sum_recv, weight_send, weight_recv,
    ) = scratch[7 * CHUNKS :]
    got, cands = (got0, got1), (cands0, cands1)
    load_query = pltpu.make_async_copy(query_hbm, query_ref, local_sem.at[2])
    load_stored = pltpu.make_async_copy(stored_hbm, stored_ref, local_sem.at[3])
    load_stored.start()
    me_dp = lax.axis_index("dp")
    y = me_dp // ROW
    member = me_dp % ROW
    up = ((y + 1) % RING) * ROW + member
    down = ((y + RING - 1) % RING) * ROW + member
    z = lax.axis_index("fsdp")
    z_targets = ((z + 1) % Z, (z + Z - 1) % Z)

    def peer_of(k):
        return (member + k) % ROW

    def row_dp(k):
        return y * ROW + peer_of(k)

    barrier = pltpu.get_barrier_semaphore()
    for target in (up, down):
        pl.semaphore_signal(barrier, inc=1, device_id={"dp": target}, device_id_type=MESH)
    for target in z_targets:
        pl.semaphore_signal(barrier, inc=1, device_id={"fsdp": target}, device_id_type=MESH)

    def greet(k, carry):
        pl.semaphore_signal(barrier, inc=1, device_id={"dp": row_dp(k)}, device_id_type=MESH)
        return carry

    lax.fori_loop(1, ROW, greet, 0)
    pl.semaphore_wait(barrier, ROW + 3)

    chunk = stored_ref.shape[1] // CHUNKS
    piece = chunk // PIECES

    def arrived(way, c, d):
        return travelling[6 * CHUNKS + c if d == 4 else (3 * way + d - 1) * CHUNKS + c]

    def piece_of(way, c, p, d):
        if d == 0:
            return stored_hbm.at[:, pl.ds(c * chunk + p * piece, piece)]
        return arrived(way, c, d).at[:, pl.ds(p * piece, piece)]

    def ring_copy(way, c, p, d):
        return pltpu.make_async_remote_copy(
            src_ref=piece_of(way, c, p, d), dst_ref=piece_of(way, c, p, d + 1),
            send_sem=ring_send.at[way, c, p, d], recv_sem=ring_recv.at[way, c, p, d],
            device_id={"dp": (up, down)[way]}, device_id_type=MESH,
        )

    def passes(way, p, d):
        return d < 3 or (d == 3 and p == way)

    ring_copies = []

    def pass_on(way, c, p, d):
        if passes(way, p, d):
            ring_copies.append(ring_copy(way, c, p, d))
            ring_copies[-1].start()

    def set_out(c):
        for p in range(PIECES):
            for way in range(2):
                pass_on(way, c, p, 0)

    def table_copy(k):
        return pltpu.make_async_remote_copy(
            src_ref=table_ref, dst_ref=tables.at[member],
            send_sem=table_send.at[k], recv_sem=table_recv.at[k],
            device_id={"dp": row_dp(k)}, device_id_type=MESH,
        )

    def start_table(k, carry):
        table_copy(k).start()
        return carry

    lax.fori_loop(1, ROW, start_table, 0)
    own_table = pltpu.make_async_copy(table_ref, tables.at[member], local_sem.at[0])
    own_table.start()
    set_out(0)
    load_query.start()

    def wait_table(k, carry):
        table_copy(k).wait()
        return carry

    lax.fori_loop(1, ROW, wait_table, 0)
    own_table.wait()
    to_smem = pltpu.make_async_copy(tables, table_smem, local_sem.at[1])
    to_smem.start()
    to_smem.wait()

    def slot_copy(group, c, k, size):
        first = (group - 1) * 2 * ROW + 2 * member if size == 2 else (6 + group // 4) * ROW + member
        return pltpu.make_async_remote_copy(
            src_ref=stage.at[group, c, k, pl.ds(0, size)], dst_ref=got[c].at[pl.ds(first, size)],
            send_sem=slot_send.at[group, c, k], recv_sem=slot_recv.at[group, c, k],
            device_id={"dp": row_dp(k)}, device_id_type=MESH,
        )

    def serve(group, c, sources):
        size = len(sources)

        def picked(k, way):
            delta, picked_from = sources[way]
            owner_y = (y + RING - delta) % RING
            return picked_from(table_smem[peer_of(k), member, owner_y])

        def send_one(k, carry):
            for way in range(size):
                stage[group, c, k, way] = picked(k, way)
            slot_copy(group, c, k, size).start()
            return carry

        lax.fori_loop(1, ROW, send_one, 0)
        first = (group - 1) * 2 * ROW + 2 * member if size == 2 else (6 + group // 4) * ROW + member
        for way in range(size):
            got[c][first + way] = picked(0, way)

    share, width = weight_own.shape
    features = query_ref.shape[1]
    list_len = width // (CHUNKS * chunk)
    part_width = width // CHUNKS
    half_width, half_share = part_width // 2, share // 2
    copies = []

    def collect(c):
        def place(i, carry):
            cands[c][i] = got[c][slots_ref[i]]
            return carry

        for group in range(5):

            def wait_slot(k, carry):
                slot_copy(group, c, k, 2 if group % 4 else 1).wait()
                return carry

            lax.fori_loop(1, ROW, wait_slot, 0)

        lax.fori_loop(0, cands[c].shape[0], place, 0)

    def listed(v, c):
        return cands[c][pl.ds((v // 2) * list_len, list_len)].reshape(part_width, features)

    def rows_of(v):
        return pl.ds(pl.multiple_of(v * share, share), share)

    def partial(c, offset):
        v = (z + offset) % Z
        value = lax.dot_general(
            query_ref[rows_of(v), :], listed(v, c), (((1,), (1,)), ((), ())),
            preferred_element_type=jnp.float32,
        )
        return (value[:, :half_width], value[:, half_width:])

    def sum_copy(c, way, dist, half):
        index = (c, way, dist - 1, half)
        return pltpu.make_async_remote_copy(
            src_ref=sums_out.at[index], dst_ref=sums_in.at[index],
            send_sem=sum_send.at[index], recv_sem=sum_recv.at[index],
            device_id={"fsdp": z_targets[way]}, device_id_type=MESH,
        )

    def send_sum(c, way, dist, half, value):
        sums_out[c, way, dist - 1, half] = value
        copies.append(sum_copy(c, way, dist, half))
        copies[-1].start()

    order = [(0, 0), (1, 1), (1, 0), (0, 1)]

    def sum_step(c, dist):
        values = (partial(c, dist), partial(c, Z - dist) if dist < 4 else None)
        if dist == 4:
            send_sum(c, 0, 4, 0, values[0][0])
            send_sum(c, 1, 4, 1, values[0][1])
            return
        for way, half in order[2:] + order[:2] if dist == 3 else order:
            value = values[way][half]
            if dist < 3 or way == half:
                sum_copy(c, way, dist + 1, half).wait_recv()
                value = value + sums_in[c, way, dist, half]
            send_sum(c, way, dist, half, value)

    def sum_end(c):
        halves = list(partial(c, 0))
        for way, half in order:
            sum_copy(c, way, 1, half).wait_recv()
            halves[half] = halves[half] + sums_in[c, way, 0, half]
        return halves

    load_stored.wait()
    for c in range(CHUNKS):
        serve(0, c, [(0, lambda chosen: stored_ref[chosen, pl.ds(c * chunk, chunk)])])
    for c in range(CHUNKS):
        for d in range(1, 5):
            for p in range(PIECES):
                for way in range(2):
                    if passes(way, p, d - 1):
                        ring_copy(way, c, p, d - 1).wait_recv()
                        pass_on(way, c, p, d)
            if c == 0 and d == 3:
                set_out(1)
            shards_in = [arrived(way, c, d) for way in range(2 if d < 4 else 1)]
            serve(
                d, c,
                [
                    (RING - d if way else d, lambda chosen, shard=shard: shard[chosen])
                    for way, shard in enumerate(shards_in)
                ],
            )
            if c == 1 and d == 2:
                load_query.wait()
                collect(0)
                sum_step(0, 4)
            if c == 1 and d == 3:
                sum_step(0, 3)
    sum_step(0, 2)
    sum_step(0, 1)
    halves = sum_end(0)
    collect(1)
    for dist in (4, 3, 2, 1):
        sum_step(1, dist)
    scores = jnp.concatenate(halves + sum_end(1), axis=1) * 50.0
    column = lax.broadcasted_iota(jnp.int32, scores.shape, 1)
    position = (
        (column % part_width // chunk) * (CHUNKS * chunk)
        + (column // part_width) * chunk
        + column % chunk
    )
    losses, weights = softmax_rows(scores, position == positive_ref[...])
    weight_own[...] = weights
    losses_ref[...] = losses

    def part(ref, c):
        return ref.at[pl.ds(c * half_share, half_share)]

    def weight_copy(way, step, c):
        source = weight_own if step == 0 else weight_in.at[way, step - 1]
        target = weight_far if step == 3 else weight_in.at[way, step]
        return pltpu.make_async_remote_copy(
            src_ref=part(source, c), dst_ref=part(target, c),
            send_sem=weight_send.at[way, step, c], recv_sem=weight_recv.at[way, step, c],
            device_id={"fsdp": z_targets[way]}, device_id_type=MESH,
        )

    def send_weights(way, step, c):
        copy = weight_copy(way, step, c)
        copy.start()
        copies.append(copy)

    def gradient(rows, offset):
        v = (z + offset) % Z
        value = sum(
            jnp.dot(
                rows[:, c * part_width : (c + 1) * part_width], listed(v, c),
                preferred_element_type=jnp.float32,
            )
            for c in range(CHUNKS)
        )
        grad_ref[rows_of(v), :] = (value * 50.0).astype(grad_ref.dtype)

    for c in range(2):
        for way in range(2):
            send_weights(way, 0, c)
    gradient(weights, 0)
    for step in range(1, 4):
        for c in range(2):
            for way in range(2):
                weight_copy(way, step - 1, c).wait_recv()
                if step < 3 or way == c:
                    send_weights(way, step, c)
        gradient(weight_in[0, step - 1], Z - step)
        gradient(weight_in[1, step - 1], step)
    for way in range(2):
        weight_copy(way, 3, way).wait_recv()
    gradient(weight_far[...], 4)
    for copy in copies + ring_copies:
        copy.wait_send()


def loss_and_gradient(slots, table, positive_rows, query, stored):
    block_rows, features = stored.shape[1:]
    share = positive_rows.shape[0]
    width = slots.shape[0] * block_rows * block_rows // query.shape[0]
    vmem = pl.BlockSpec(memory_space=pltpu.VMEM)
    hbm = pl.BlockSpec(memory_space=pltpu.HBM)
    travelling = pltpu.VMEM(
        (stored.shape[0], block_rows // CHUNKS, features), stored.dtype
    )
    chunk = block_rows // CHUNKS
    sums = pltpu.VMEM((CHUNKS, 2, 4, 2, share, width // CHUNKS // 2), jnp.float32)
    dma = pltpu.SemaphoreType.DMA
    return pl.pallas_call(
        loss_kernel,
        out_shape=(
            jax.ShapeDtypeStruct((share, 1), jnp.float32),
            jax.ShapeDtypeStruct(query.shape, query.dtype),
        ),
        in_specs=[pl.BlockSpec(memory_space=pltpu.SMEM), vmem, vmem, hbm, hbm],
        out_specs=(vmem, vmem),
        scratch_shapes=[travelling] * (7 * CHUNKS)
        + [
            pltpu.VMEM(query.shape, query.dtype),
            pltpu.VMEM(stored.shape, stored.dtype),
            pltpu.VMEM((5, CHUNKS, ROW, 2, chunk, features), stored.dtype),
            pltpu.VMEM((RING * ROW, chunk, features), stored.dtype),
            pltpu.VMEM((RING * ROW, chunk, features), stored.dtype),
            pltpu.VMEM((ROW,) + table.shape, jnp.int32),
            pltpu.SMEM((ROW,) + table.shape, jnp.int32),
            pltpu.VMEM((slots.shape[0], chunk, features), stored.dtype),
            pltpu.VMEM((slots.shape[0], chunk, features), stored.dtype),
            sums,
            sums,
            pltpu.VMEM((share, width), jnp.bfloat16),
            pltpu.VMEM((2, 3, share, width), jnp.bfloat16),
            pltpu.VMEM((share, width), jnp.bfloat16),
            dma((2, CHUNKS, PIECES, 4)),
            dma((2, CHUNKS, PIECES, 4)),
            dma((ROW,)),
            dma((ROW,)),
            dma((5, CHUNKS, ROW)),
            dma((5, CHUNKS, ROW)),
            dma((4,)),
            dma((CHUNKS, 2, 4, 2)),
            dma((CHUNKS, 2, 4, 2)),
            dma((2, 4, 2)),
            dma((2, 4, 2)),
        ],
        compiler_params=pltpu.CompilerParams(
            collective_id=0, has_side_effects=True, vmem_limit_bytes=48 * 1024 * 1024
        ),
        name="loss",
    )(slots, table, positive_rows, query, stored)


def shards(query_emb, passage_emb, cand_blocks, positive):
    row_count, feature_count = query_emb.shape
    block_rows = row_count // cand_blocks.shape[0]
    passage_blocks = passage_emb.shape[0] // block_rows
    wanted = cand_blocks.reshape(-1)
    owners = wanted // passage_blocks
    local_ids = wanted % passage_blocks
    owner_y = owners // ROW
    owner_member = owners % ROW
    at_member = owner_member[:, None, None] == lax.broadcasted_iota(jnp.int32, (1, ROW, 128), 1)
    at_row = owner_y[:, None, None] == lax.broadcasted_iota(jnp.int32, (1, ROW, 128), 2)
    table = jnp.sum(jnp.where(at_member & at_row, local_ids[:, None, None], 0), axis=0)
    my_y = lax.axis_index("dp") // ROW
    delta = (my_y - owner_y + RING) % RING
    pair = jnp.minimum(delta, RING - delta)
    slots = jnp.where(
        pair % 4 == 0,
        (6 + pair // 4) * ROW + owner_member,
        ((pair - 1) * ROW + owner_member) * 2 + (delta > 4),
    )
    share = row_count // Z
    first_row = lax.axis_index("fsdp") * share
    positive_rows = lax.dynamic_slice_in_dim(positive, first_row, share)[:, None]
    stored = passage_emb.reshape(passage_blocks, block_rows, feature_count)
    losses, query_grad = loss_and_gradient(slots, table, positive_rows, query_emb, stored)
    return (losses[:, 0], query_grad)


def solution(mesh):
    return jax.shard_map(
        shards,
        mesh=mesh,
        in_specs=(P("dp", "fsdp"), P("dp", "fsdp"), P("dp", None), P("dp")),
        out_specs=(P(("dp", "fsdp")), P("dp", "fsdp")),
        check_vma=False,
    )
```

```python
import jax
import jax.numpy as jnp
from jax import lax
from jax.experimental import pallas as pl
from jax.experimental.pallas import tpu as pltpu
from jax.sharding import PartitionSpec as P

MESH = pl.DeviceIdType.MESH
RING = 8
ROW = 8
Z = 8
CHUNKS = 2
PIECES = 2


def softmax_rows(scores, matched):
    row_max = jnp.max(scores, axis=1, keepdims=True)
    log_total = row_max + jnp.log(jnp.sum(jnp.exp(scores - row_max), axis=1, keepdims=True))
    losses = log_total - jnp.sum(
        jnp.where(matched, scores, jnp.float32(0.0)), axis=1, keepdims=True
    )
    weights = (jnp.exp(scores - log_total) - matched.astype(jnp.float32)).astype(jnp.bfloat16)
    return (losses, weights)


def loss_kernel(
    slots_ref, table_ref, positive_ref, query_hbm, stored_hbm, losses_ref, grad_ref,
    *scratch,
):
    travelling = scratch[: 7 * CHUNKS]
    (
        query_ref, stored_ref, stage, got0, got1, tables, table_smem,
        cands0, cands1, sums_out, sums_in, weight_own, weight_in, weight_far,
        ring_send, ring_recv, table_send, table_recv, slot_send, slot_recv, local_sem,
        sum_send, sum_recv, weight_send, weight_recv,
    ) = scratch[7 * CHUNKS :]
    got, cands = (got0, got1), (cands0, cands1)
    load_query = pltpu.make_async_copy(query_hbm, query_ref, local_sem.at[2])
    load_stored = pltpu.make_async_copy(stored_hbm, stored_ref, local_sem.at[3])
    load_stored.start()
    me_dp = lax.axis_index("dp")
    y = me_dp // ROW
    member = me_dp % ROW
    up = ((y + 1) % RING) * ROW + member
    down = ((y + RING - 1) % RING) * ROW + member
    z = lax.axis_index("fsdp")
    z_targets = ((z + 1) % Z, (z + Z - 1) % Z)

    def peer_of(k):
        return (member + k) % ROW

    def row_dp(k):
        return y * ROW + peer_of(k)

    barrier = pltpu.get_barrier_semaphore()
    for target in (up, down):
        pl.semaphore_signal(barrier, inc=1, device_id={"dp": target}, device_id_type=MESH)
    for target in z_targets:
        pl.semaphore_signal(barrier, inc=1, device_id={"fsdp": target}, device_id_type=MESH)

    def greet(k, carry):
        pl.semaphore_signal(barrier, inc=1, device_id={"dp": row_dp(k)}, device_id_type=MESH)
        return carry

    lax.fori_loop(1, ROW, greet, 0)
    pl.semaphore_wait(barrier, ROW + 3)

    chunk = stored_ref.shape[1] // CHUNKS
    piece = chunk // PIECES

    def arrived(way, c, d):
        return travelling[6 * CHUNKS + c if d == 4 else (3 * way + d - 1) * CHUNKS + c]

    def piece_of(way, c, p, d):
        if d == 0:
            return stored_hbm.at[:, pl.ds(c * chunk + p * piece, piece)]
        return arrived(way, c, d).at[:, pl.ds(p * piece, piece)]

    def ring_copy(way, c, p, d):
        return pltpu.make_async_remote_copy(
            src_ref=piece_of(way, c, p, d), dst_ref=piece_of(way, c, p, d + 1),
            send_sem=ring_send.at[way, c, p, d], recv_sem=ring_recv.at[way, c, p, d],
            device_id={"dp": (up, down)[way]}, device_id_type=MESH,
        )

    def passes(way, p, d):
        return d < 3 or (d == 3 and p == way)

    ring_copies = []

    def pass_on(way, c, p, d):
        if passes(way, p, d):
            ring_copies.append(ring_copy(way, c, p, d))
            ring_copies[-1].start()

    def set_out(c):
        for p in range(PIECES):
            for way in range(2):
                pass_on(way, c, p, 0)

    def table_copy(k):
        return pltpu.make_async_remote_copy(
            src_ref=table_ref, dst_ref=tables.at[member],
            send_sem=table_send.at[k], recv_sem=table_recv.at[k],
            device_id={"dp": row_dp(k)}, device_id_type=MESH,
        )

    def start_table(k, carry):
        table_copy(k).start()
        return carry

    lax.fori_loop(1, ROW, start_table, 0)
    own_table = pltpu.make_async_copy(table_ref, tables.at[member], local_sem.at[0])
    own_table.start()
    set_out(0)
    load_query.start()

    def wait_table(k, carry):
        table_copy(k).wait()
        return carry

    lax.fori_loop(1, ROW, wait_table, 0)
    own_table.wait()
    to_smem = pltpu.make_async_copy(tables, table_smem, local_sem.at[1])
    to_smem.start()
    to_smem.wait()

    def slot_copy(group, c, k, size):
        first = (group - 1) * 2 * ROW + 2 * member if size == 2 else (6 + group // 4) * ROW + member
        return pltpu.make_async_remote_copy(
            src_ref=stage.at[group, c, k, pl.ds(0, size)], dst_ref=got[c].at[pl.ds(first, size)],
            send_sem=slot_send.at[group, c, k], recv_sem=slot_recv.at[group, c, k],
            device_id={"dp": row_dp(k)}, device_id_type=MESH,
        )

    def serve(group, c, sources):
        size = len(sources)

        def picked(k, way):
            delta, picked_from = sources[way]
            owner_y = (y + RING - delta) % RING
            return picked_from(table_smem[peer_of(k), member, owner_y])

        def send_one(k, carry):
            for way in range(size):
                stage[group, c, k, way] = picked(k, way)
            slot_copy(group, c, k, size).start()
            return carry

        lax.fori_loop(1, ROW, send_one, 0)
        first = (group - 1) * 2 * ROW + 2 * member if size == 2 else (6 + group // 4) * ROW + member
        for way in range(size):
            got[c][first + way] = picked(0, way)

    share, width = weight_own.shape
    features = query_ref.shape[1]
    list_len = width // (CHUNKS * chunk)
    part_width = width // CHUNKS
    half_width, half_share = part_width // 2, share // 2
    copies = []

    def collect(c):
        def place(i, carry):
            cands[c][i] = got[c][slots_ref[i]]
            return carry

        for group in range(5):

            def wait_slot(k, carry):
                slot_copy(group, c, k, 2 if group % 4 else 1).wait()
                return carry

            lax.fori_loop(1, ROW, wait_slot, 0)

        lax.fori_loop(0, cands[c].shape[0], place, 0)

    def listed(v, c):
        return cands[c][pl.ds((v // 2) * list_len, list_len)].reshape(part_width, features)

    def rows_of(v):
        return pl.ds(pl.multiple_of(v * share, share), share)

    def partial(c, offset):
        v = (z + offset) % Z
        value = lax.dot_general(
            query_ref[rows_of(v), :], listed(v, c), (((1,), (1,)), ((), ())),
            preferred_element_type=jnp.float32,
        )
        return (value[:, :half_width], value[:, half_width:])

    def sum_copy(c, way, dist, half):
        index = (c, way, dist - 1, half)
        return pltpu.make_async_remote_copy(
            src_ref=sums_out.at[index], dst_ref=sums_in.at[index],
            send_sem=sum_send.at[index], recv_sem=sum_recv.at[index],
            device_id={"fsdp": z_targets[way]}, device_id_type=MESH,
        )

    def send_sum(c, way, dist, half, value):
        sums_out[c, way, dist - 1, half] = value
        copies.append(sum_copy(c, way, dist, half))
        copies[-1].start()

    order = [(0, 0), (1, 1), (1, 0), (0, 1)]

    def sum_step(c, dist):
        values = (partial(c, dist), partial(c, Z - dist) if dist < 4 else None)
        if dist == 4:
            send_sum(c, 0, 4, 0, values[0][0])
            send_sum(c, 1, 4, 1, values[0][1])
            return
        for way, half in order[2:] + order[:2] if dist == 3 else order:
            value = values[way][half]
            if dist < 3 or way == half:
                sum_copy(c, way, dist + 1, half).wait_recv()
                value = value + sums_in[c, way, dist, half]
            send_sum(c, way, dist, half, value)

    def sum_end(c):
        halves = list(partial(c, 0))
        for way, half in order:
            sum_copy(c, way, 1, half).wait_recv()
            halves[half] = halves[half] + sums_in[c, way, 0, half]
        return halves

    load_stored.wait()
    for c in range(CHUNKS):
        serve(0, c, [(0, lambda chosen: stored_ref[chosen, pl.ds(c * chunk, chunk)])])
    for c in range(CHUNKS):
        for d in range(1, 5):
            for p in range(PIECES):
                for way in range(2):
                    if passes(way, p, d - 1):
                        ring_copy(way, c, p, d - 1).wait_recv()
                        pass_on(way, c, p, d)
            if c == 0 and d == 3:
                set_out(1)
            shards_in = [arrived(way, c, d) for way in range(2 if d < 4 else 1)]
            serve(
                d, c,
                [
                    (RING - d if way else d, lambda chosen, shard=shard: shard[chosen])
                    for way, shard in enumerate(shards_in)
                ],
            )
            if c == 1 and d == 2:
                load_query.wait()
                collect(0)
                sum_step(0, 4)
            if c == 1 and d == 3:
                sum_step(0, 3)
    sum_step(0, 2)
    sum_step(0, 1)
    halves = sum_end(0)
    collect(1)
    for dist in (4, 3, 2, 1):
        sum_step(1, dist)
    scores = jnp.concatenate(halves + sum_end(1), axis=1) * 50.0
    column = lax.broadcasted_iota(jnp.int32, scores.shape, 1)
    position = (
        (column % part_width // chunk) * (CHUNKS * chunk)
        + (column // part_width) * chunk
        + column % chunk
    )
    losses, weights = softmax_rows(scores, position == positive_ref[...])
    weight_own[...] = weights
    square = (share, share)
    diagonal = lax.broadcasted_iota(jnp.int32, square, 0) == lax.broadcasted_iota(
        jnp.int32, square, 1
    )
    losses_ref[...] = jnp.sum(jnp.where(diagonal, losses, 0.0), axis=0, keepdims=True)

    def part(ref, c):
        return ref.at[pl.ds(c * half_share, half_share)]

    def weight_copy(way, step, c):
        source = weight_own if step == 0 else weight_in.at[way, step - 1]
        target = weight_far if step == 3 else weight_in.at[way, step]
        return pltpu.make_async_remote_copy(
            src_ref=part(source, c), dst_ref=part(target, c),
            send_sem=weight_send.at[way, step, c], recv_sem=weight_recv.at[way, step, c],
            device_id={"fsdp": z_targets[way]}, device_id_type=MESH,
        )

    def send_weights(way, step, c):
        copy = weight_copy(way, step, c)
        copy.start()
        copies.append(copy)

    def gradient(rows, offset):
        v = (z + offset) % Z
        value = sum(
            jnp.dot(
                rows[:, c * part_width : (c + 1) * part_width], listed(v, c),
                preferred_element_type=jnp.float32,
            )
            for c in range(CHUNKS)
        )
        grad_ref[rows_of(v), :] = (value * 50.0).astype(grad_ref.dtype)

    for c in range(2):
        for way in range(2):
            send_weights(way, 0, c)
    gradient(weights, 0)
    for step in range(1, 4):
        for c in range(2):
            for way in range(2):
                weight_copy(way, step - 1, c).wait_recv()
                if step < 3 or way == c:
                    send_weights(way, step, c)
        gradient(weight_in[0, step - 1], Z - step)
        gradient(weight_in[1, step - 1], step)
    for way in range(2):
        weight_copy(way, 3, way).wait_recv()
    gradient(weight_far[...], 4)
    for copy in copies + ring_copies:
        copy.wait_send()


def loss_and_gradient(slots, table, positive_rows, query, stored):
    block_rows, features = stored.shape[1:]
    share = positive_rows.shape[0]
    width = slots.shape[0] * block_rows * block_rows // query.shape[0]
    vmem = pl.BlockSpec(memory_space=pltpu.VMEM)
    hbm = pl.BlockSpec(memory_space=pltpu.HBM)
    travelling = pltpu.VMEM(
        (stored.shape[0], block_rows // CHUNKS, features), stored.dtype
    )
    chunk = block_rows // CHUNKS
    sums = pltpu.VMEM((CHUNKS, 2, 4, 2, share, width // CHUNKS // 2), jnp.float32)
    dma = pltpu.SemaphoreType.DMA
    return pl.pallas_call(
        loss_kernel,
        out_shape=(
            jax.ShapeDtypeStruct((1, share), jnp.float32),
            jax.ShapeDtypeStruct(query.shape, query.dtype),
        ),
        in_specs=[pl.BlockSpec(memory_space=pltpu.SMEM), vmem, vmem, hbm, hbm],
        out_specs=(vmem, vmem),
        scratch_shapes=[travelling] * (7 * CHUNKS)
        + [
            pltpu.VMEM(query.shape, query.dtype),
            pltpu.VMEM(stored.shape, stored.dtype),
            pltpu.VMEM((5, CHUNKS, ROW, 2, chunk, features), stored.dtype),
            pltpu.VMEM((RING * ROW, chunk, features), stored.dtype),
            pltpu.VMEM((RING * ROW, chunk, features), stored.dtype),
            pltpu.VMEM((ROW,) + table.shape, jnp.int32),
            pltpu.SMEM((ROW,) + table.shape, jnp.int32),
            pltpu.VMEM((slots.shape[0], chunk, features), stored.dtype),
            pltpu.VMEM((slots.shape[0], chunk, features), stored.dtype),
            sums,
            sums,
            pltpu.VMEM((share, width), jnp.bfloat16),
            pltpu.VMEM((2, 3, share, width), jnp.bfloat16),
            pltpu.VMEM((share, width), jnp.bfloat16),
            dma((2, CHUNKS, PIECES, 4)),
            dma((2, CHUNKS, PIECES, 4)),
            dma((ROW,)),
            dma((ROW,)),
            dma((5, CHUNKS, ROW)),
            dma((5, CHUNKS, ROW)),
            dma((4,)),
            dma((CHUNKS, 2, 4, 2)),
            dma((CHUNKS, 2, 4, 2)),
            dma((2, 4, 2)),
            dma((2, 4, 2)),
        ],
        compiler_params=pltpu.CompilerParams(
            collective_id=0, has_side_effects=True, vmem_limit_bytes=48 * 1024 * 1024
        ),
        name="loss",
    )(slots, table, positive_rows, query, stored)


def shards(query_emb, passage_emb, cand_blocks, positive):
    row_count, feature_count = query_emb.shape
    block_rows = row_count // cand_blocks.shape[0]
    passage_blocks = passage_emb.shape[0] // block_rows
    wanted = cand_blocks.reshape(-1)
    owners = wanted // passage_blocks
    local_ids = wanted % passage_blocks
    owner_y = owners // ROW
    owner_member = owners % ROW
    at_member = owner_member[:, None, None] == lax.broadcasted_iota(jnp.int32, (1, ROW, 128), 1)
    at_row = owner_y[:, None, None] == lax.broadcasted_iota(jnp.int32, (1, ROW, 128), 2)
    table = jnp.sum(jnp.where(at_member & at_row, local_ids[:, None, None], 0), axis=0)
    my_y = lax.axis_index("dp") // ROW
    delta = (my_y - owner_y + RING) % RING
    pair = jnp.minimum(delta, RING - delta)
    slots = jnp.where(
        pair % 4 == 0,
        (6 + pair // 4) * ROW + owner_member,
        ((pair - 1) * ROW + owner_member) * 2 + (delta > 4),
    )
    share = row_count // Z
    first_row = lax.axis_index("fsdp") * share
    positive_rows = lax.dynamic_slice_in_dim(positive, first_row, share)[:, None]
    stored = passage_emb.reshape(passage_blocks, block_rows, feature_count)
    losses, query_grad = loss_and_gradient(slots, table, positive_rows, query_emb, stored)
    return (losses[0], query_grad)


def solution(mesh):
    return jax.shard_map(
        shards,
        mesh=mesh,
        in_specs=(P("dp", "fsdp"), P("dp", "fsdp"), P("dp", None), P("dp")),
        out_specs=(P(("dp", "fsdp")), P("dp", "fsdp")),
        check_vma=False,
    )
```
